128 devices in a mesh: section: 2 (over x_hi), expert: 16 (over y, z), replica: 4 (over x_lo, core).
Axes of the slice: x: 4 (x_hi: 2, x_lo: 2; x = x_hi * 2 + x_lo), y: 4, z: 4, core: 2. Of those that a mesh axis runs over, the one named last changes fastest.
Arguments:
- boundary: bfloat16 [2, 2, 128, 50, 768], P('section', None, ('expert', 'replica')), may hold values from -6 to 6
- routes: int32 [2, 2, 128, 50, 2], P('section', None, ('expert', 'replica')), may hold values from 0 to 31, all different within a row; in each aligned block of 100 rows (0 to 99, 100 to 199, ..., all dimensions but the last counted through in order) at most 9 rows name the same one
- norm_gains: bfloat16 [2, 2, 768], P('section', None, 'expert'), may hold values from 0.25 to 1.75
- norm_biases: bfloat16 [2, 2, 768], P('section', None, 'expert'), may hold values from -3 to 3
- attend_weight: bfloat16 [2, 768, 2304], P('section', 'expert'), may hold values from -0.21875 to 0.21875
- output_weight: bfloat16 [2, 768, 768], P('section', 'expert'), may hold values from -0.875 to 0.875
- router_weight: bfloat16 [2, 768, 32], P('section', 'expert'), may hold values from -0.21875 to 0.21875
- expert_in: bfloat16 [2, 32, 768, 3072], P('section', 'expert', None, 'replica'), may hold values from -0.21875 to 0.21875
- expert_out: bfloat16 [2, 32, 3072, 768], P('section', 'expert', 'replica'), may hold values from -0.15625 to 0.15625
Outputs:
- results: bfloat16 [2, 2, 128, 50, 768], P('section', None, ('expert', 'replica'))
- gains_grad: float32 [2, 2, 768], P('section', None, 'expert')
- biases_grad: float32 [2, 2, 768], P('section', None, 'expert')
- attend_grad: float32 [2, 768, 2304], P('section', 'expert')
- output_grad: float32 [2, 768, 768], P('section', 'expert')
- router_grad: float32 [2, 768, 32], P('section', 'expert')
- expert_in_grad: float32 [2, 32, 768, 3072], P('section', 'expert', None, 'replica')
- expert_out_grad: float32 [2, 32, 3072, 768], P('section', 'expert', 'replica')
The draws below stay inside these ranges and needn't reach their ends.
Inputs may be any that keep to these rules, and one draw needn't show every extreme that they name: `routes`: in each layer and micro-batch, the rows of one data index (2 images, both choices) name any one expert at most 9 times, and some expert reaches 9; a token's two experts differ.
All inputs are finite; a program needn't handle non-finite values.
Results may differ from the reference program's by a relative error of at most 0.029.
Values may be sent and summed in bfloat16 or wider, within the bound.
A program may use at most 192 MiB of HBM per device.

```python
import math
import jax
import jax.numpy as jnp
import numpy as np
from jax import lax

D = 768
HEADS = 12
HEAD_DIM = 64
H = 3072
S = 50
IMG_DEV = 2
M = 2
EXPERTS = 32
IMAGES_MB = 128
CAP = 9


def steps_of(rng, dims, cuts, smallest, largest):
    gain, own = 1.0, jax.random.fold_in(rng, 6)
    for position, parts in cuts:
        steps = jnp.exp(jax.random.uniform(jax.random.fold_in(own, position), (parts,), jnp.float32, smallest / len(cuts), largest / len(cuts)))
        gain = gain * jnp.repeat(steps, dims[position] // parts).reshape([-1 if axis == position else 1 for axis in range(len(dims))])
    return gain


def deal_out(key, own, number, rows, number_of, top, limit, skew):
    ranking = jax.random.permutation(key, number_of)
    crowded, usual = load_shares(number_of, rows * top, limit, skew, True), load_shares(number_of, rows * top, limit, skew, False)
    places = jnp.arange(number_of)

    def named(lengths, offset_by):
        used = int((lengths > 0).sum())
        fixed = max(1, used // 4)
        moved = fixed + (places - fixed + offset_by * (used - fixed)) % max(1, number_of - fixed)
        return jnp.zeros((number_of,), jnp.int32).at[ranking[jnp.where(places < fixed, places, moved)]].set(jnp.asarray(lengths, jnp.int32))

    lengths = jnp.where(number % 4 == 0, named(crowded, number // 4), named(usual, number - number // 4 - 1))
    mixed = jax.random.permutation(jax.random.fold_in(own, 3), number_of)
    donor, taker = mixed[0:number_of // 2 * 2:2], mixed[1:number_of // 2 * 2:2]
    margin = jnp.minimum(lengths[donor] - 1, limit - lengths[taker]) // 2
    margin = jnp.where((donor == ranking[0]) | (taker == ranking[0]) | (lengths[taker] == 0), 0, jnp.maximum(margin, 0))
    moved = jax.random.randint(jax.random.fold_in(own, 4), (number_of // 2,), 0, 1 << 20) % (margin + 1)
    lengths = lengths.at[donor].add(-moved).at[taker].add(moved)
    items = jnp.searchsorted(jnp.cumsum(lengths), jnp.arange(rows * top), side="right").astype(jnp.int32)
    listing = items.reshape(top, rows).T
    listing = listing[jax.random.permutation(jax.random.fold_in(own, 1), rows)]
    offset_by = jax.random.randint(jax.random.fold_in(own, 2), (rows, 1), 0, top)
    return jnp.take_along_axis(listing, (jnp.arange(top)[None, :] + offset_by) % top, axis=1)


def load_shares(number_of, total, limit, lean, full):
    portions = [(1 << 20) // math.isqrt(grade ** lean) + 1 for grade in range(1, number_of + 1)]
    largest = limit if full else min(limit, max(-(-total // number_of), total * portions[0] // sum(portions)))
    least = 1 if total - largest >= number_of - 1 else 0
    holding, spare = [largest] + [least] * (number_of - 1), total - largest - least * (number_of - 1)
    while spare > 0:
        movable = [i for i in range(1, number_of) if holding[i] < largest] or [i for i in range(1, number_of) if holding[i] < limit]
        mass, budget = sum([portions[i] for i in movable]), spare
        for i in movable:
            more = min(limit - holding[i], max(1, budget * portions[i] // mass), spare)
            holding[i] = holding[i] + more
            spare = spare - more
    return np.array(holding)


def noise(key, dims, scale, most, split=(), kind=jnp.bfloat16):
    entries = jax.random.normal(key, dims, jnp.float32) * scale
    if len(split) > 0:
        entries = steps_of(key, dims, split, -0.22, 0.18) * entries
    return jnp.clip(entries, min=-most, max=most).astype(kind)


def setup_inputs(seed: int = 0) -> dict:
    seeds = jax.random.split(jax.random.key(seed), 10)
    boundary = noise(seeds[0], (2, M, IMAGES_MB, S, D), 1.0, 6.0, ((0, 2), (2, 64)))
    routes_keys = jax.random.split(jax.random.fold_in(seeds[1], 1), 2 * M * IMAGES_MB * S // (IMG_DEV * S))
    routes_turns = jax.random.permutation(jax.random.fold_in(seeds[1], 3), 2 * M * IMAGES_MB * S // (IMG_DEV * S))
    routes = jax.vmap(lambda own, number: deal_out(jax.random.fold_in(seeds[1], 2), own, number, IMG_DEV * S, EXPERTS, 2, CAP, 2))(routes_keys, routes_turns).reshape((2, M, IMAGES_MB, S, 2))
    norm_gains = jnp.clip(1.0 + 0.15 * jax.random.normal(seeds[2], (2, 2, D), jnp.float32), 0.25, 1.75).astype(jnp.bfloat16)
    norm_biases = noise(seeds[3], (2, 2, D), 0.5, 3.0, ((0, 2), (2, 16)))
    attend_weight = noise(seeds[4], (2, D, 3 * D), D ** -0.5, 0.21875, ((0, 2), (1, 16)))
    output_weight = noise(seeds[5], (2, D, D), (D // 16) ** -0.5, 0.875, ((0, 2), (1, 16)))
    router_weight = noise(seeds[6], (2, D, EXPERTS), D ** -0.5, 0.21875, ((0, 2), (1, 16)))
    expert_in = noise(seeds[7], (2, EXPERTS, D, H), D ** -0.5, 0.21875, ((0, 2), (1, 16), (3, 4)))
    expert_out = noise(seeds[8], (2, EXPERTS, H, D), (H // 2) ** -0.5, 0.15625, ((0, 2), (1, 16), (2, 4)))
    return dict(boundary=boundary, routes=routes, norm_gains=norm_gains, norm_biases=norm_biases, attend_weight=attend_weight, output_weight=output_weight, router_weight=router_weight, expert_in=expert_in, expert_out=expert_out)


EPSILON = 1e-06

def norm_apply(inputs, gain_vec, bias_vec):
    centre = lax.optimization_barrier(jnp.mean(inputs, axis=-1, keepdims=True))
    spread = lax.optimization_barrier(jnp.mean(jnp.square(inputs - centre), axis=-1, keepdims=True))
    return (inputs - centre) * lax.rsqrt(spread + EPSILON) * gain_vec + bias_vec

def gelu_tanh(pre_act):
    return jax.nn.gelu(pre_act, approximate=True)

def slot_table(route_ids):
    onehot = (route_ids[..., None] == jnp.arange(EXPERTS, dtype=jnp.int32)).astype(jnp.int32)
    flatten = onehot.reshape(onehot.shape[0], -1, EXPERTS)
    before = jnp.cumsum(flatten, axis=1) - flatten
    return lax.optimization_barrier(jnp.sum(before * flatten, axis=-1)).reshape(route_ids.shape)

def split_heads(joint_proj, images):
    queries = joint_proj[:, :D].reshape(images, S, HEADS, HEAD_DIM).astype(jnp.float32)
    keys_in = joint_proj[:, D:2 * D].reshape(images, S, HEADS, HEAD_DIM).astype(jnp.float32)
    values = joint_proj[:, 2 * D:].reshape(images, S, HEADS, HEAD_DIM).astype(jnp.float32)
    return (queries, keys_in, values)

def layer_forward(params, tokens, route_ids):
    gain_rows, bias_rows, attend_w, output_w, router_w, weight_in, weight_out = params
    images = tokens.shape[0]
    row_count = images * S
    scaling = 1.0 / math.sqrt(HEAD_DIM)
    inputs = tokens.reshape(row_count, D).astype(jnp.float32)
    normed_one = norm_apply(inputs, gain_rows[0].astype(jnp.float32), bias_rows[0].astype(jnp.float32)).astype(jnp.bfloat16)
    joint_proj = jnp.dot(normed_one, attend_w, preferred_element_type=jnp.float32).astype(jnp.bfloat16)
    queries, keys_in, values = split_heads(joint_proj, images)
    scores = jnp.einsum('nqhc,nkhc->nhqk', queries, keys_in) * scaling
    row_max = lax.optimization_barrier(jnp.max(scores, axis=-1, keepdims=True))
    raised = jnp.exp(scores - row_max)
    row_total = lax.optimization_barrier(jnp.sum(raised, axis=-1, keepdims=True))
    log_total = row_max + jnp.log(row_total)
    attn_prob = (raised / row_total).astype(jnp.bfloat16)
    mixed_heads = jnp.einsum('nhqk,nkhc->nqhc', attn_prob.astype(jnp.float32), values)
    mixed_heads = mixed_heads.reshape(row_count, D).astype(jnp.bfloat16)
    hidden = inputs + jnp.dot(mixed_heads, output_w, preferred_element_type=jnp.float32)
    normed_two = norm_apply(hidden, gain_rows[1].astype(jnp.float32), bias_rows[1].astype(jnp.float32)).astype(jnp.bfloat16)
    logits = jnp.dot(normed_two, router_w, preferred_element_type=jnp.float32)
    flat_routes = route_ids.reshape(row_count, 2)
    chosen = jnp.take_along_axis(logits, flat_routes, axis=1)
    gate_vals = jax.nn.softmax(chosen, axis=-1)
    block_rows = IMG_DEV * S
    blocks = row_count // block_rows
    slot_at = slot_table(flat_routes.reshape(blocks, block_rows, 2)).reshape(row_count, 2)
    block_of = jnp.broadcast_to((jnp.arange(row_count, dtype=jnp.int32) // block_rows)[:, None], (row_count, 2))
    buffer = jnp.zeros((EXPERTS, blocks, CAP, D), jnp.bfloat16)
    buffer = buffer.at[flat_routes, block_of, slot_at].set(jnp.broadcast_to(normed_two[:, None, :], (row_count, 2, D)))

    def expert_forward(packed):
        slab_rows, first_mat, second_mat = packed
        pre_act = jnp.dot(slab_rows.reshape(-1, D), first_mat, preferred_element_type=jnp.float32)
        active = gelu_tanh(pre_act).astype(jnp.bfloat16)
        produced = jnp.dot(active, second_mat, preferred_element_type=jnp.float32).astype(jnp.bfloat16)
        return (pre_act, produced)
    pre_all, out_all = lax.map(expert_forward, (buffer, weight_in, weight_out))
    out_all = out_all.reshape(EXPERTS, blocks, CAP, D)
    expert_rows = out_all[flat_routes, block_of, slot_at]
    output = hidden + lax.optimization_barrier(jnp.sum(gate_vals[:, :, None] * expert_rows.astype(jnp.float32), axis=1))
    stored = dict(inputs=inputs, normed_one=normed_one, joint_proj=joint_proj, log_total=log_total, mixed_heads=mixed_heads, hidden=hidden, normed_two=normed_two, gate_vals=gate_vals, expert_rows=expert_rows, flat_routes=flat_routes, block_of=block_of, slot_at=slot_at, buffer=buffer, pre_all=pre_all)
    return (output, stored)

def layer_backward(params, stored, cotangent):
    gain_rows, bias_rows, attend_w, output_w, router_w, weight_in, weight_out = params
    row_count = cotangent.shape[0]
    images = row_count // S
    scaling = 1.0 / math.sqrt(HEAD_DIM)
    gate_vals = stored['gate_vals']
    flat_routes = stored['flat_routes']
    block_of = stored['block_of']
    slot_at = stored['slot_at']
    blocks = stored['buffer'].shape[1]
    send_rows = (gate_vals[:, :, None] * cotangent[:, None, :]).astype(jnp.bfloat16)
    gate_grad = lax.optimization_barrier(jnp.sum(cotangent[:, None, :] * stored['expert_rows'].astype(jnp.float32), axis=-1))
    chosen_grad = gate_vals * (gate_grad - lax.optimization_barrier(jnp.sum(gate_vals * gate_grad, axis=-1, keepdims=True)))
    onehot = (flat_routes[:, :, None] == jnp.arange(EXPERTS, dtype=jnp.int32)).astype(jnp.float32)
    logit_grad = lax.optimization_barrier(jnp.sum(chosen_grad[:, :, None] * onehot, axis=1)).astype(jnp.bfloat16)
    router_g = jnp.dot(stored['normed_two'].T, logit_grad, preferred_element_type=jnp.float32)
    router_part = jnp.dot(logit_grad, router_w.T, preferred_element_type=jnp.float32)
    grad_buffer = jnp.zeros((EXPERTS, blocks, CAP, D), jnp.bfloat16)
    grad_buffer = grad_buffer.at[flat_routes, block_of, slot_at].set(send_rows)

    def expert_backward(packed):
        slab_rows, grad_slab, pre_act, first_mat, second_mat = packed
        slab_flat = slab_rows.reshape(-1, D)
        grad_flat = grad_slab.reshape(-1, D)
        active = gelu_tanh(pre_act).astype(jnp.bfloat16)
        act_grad = jnp.dot(grad_flat, second_mat.T, preferred_element_type=jnp.float32)
        pre_grad = jax.vjp(gelu_tanh, pre_act)[1](act_grad)[0].astype(jnp.bfloat16)
        first_g = jnp.dot(slab_flat.T, pre_grad, preferred_element_type=jnp.float32)
        second_g = jnp.dot(active.T, grad_flat, preferred_element_type=jnp.float32)
        back = jnp.dot(pre_grad, first_mat.T, preferred_element_type=jnp.float32).astype(jnp.bfloat16)
        return (first_g, second_g, back)
    first_all, second_all, back_all = lax.map(expert_backward, (stored['buffer'], grad_buffer, stored['pre_all'], weight_in, weight_out))
    back_rows = back_all.reshape(EXPERTS, blocks, CAP, D)[flat_routes, block_of, slot_at]
    normed_grad = router_part + lax.optimization_barrier(jnp.sum(back_rows.astype(jnp.float32), axis=1))
    pull_two = jax.vjp(norm_apply, stored['hidden'], gain_rows[1].astype(jnp.float32), bias_rows[1].astype(jnp.float32))[1]
    hidden_part, gain_two, bias_two = pull_two(normed_grad)
    hidden_grad = cotangent + hidden_part
    hidden_b = hidden_grad.astype(jnp.bfloat16)
    output_g = jnp.dot(stored['mixed_heads'].T, hidden_b, preferred_element_type=jnp.float32)
    mixed_grad = jnp.dot(hidden_b, output_w.T, preferred_element_type=jnp.float32).astype(jnp.bfloat16)
    mixed_grad = mixed_grad.reshape(images, S, HEADS, HEAD_DIM).astype(jnp.float32)
    queries, keys_in, values = split_heads(stored['joint_proj'], images)
    scores = jnp.einsum('nqhc,nkhc->nhqk', queries, keys_in) * scaling
    attn_prob = jnp.exp(scores - stored['log_total'])
    prob_b = attn_prob.astype(jnp.bfloat16).astype(jnp.float32)
    value_grad = jnp.einsum('nhqk,nqhc->nkhc', prob_b, mixed_grad)
    prob_grad = jnp.einsum('nqhc,nkhc->nhqk', mixed_grad, values)
    row_delta = lax.optimization_barrier(jnp.sum(attn_prob * prob_grad, axis=-1, keepdims=True))
    score_grad = (attn_prob * (prob_grad - row_delta) * scaling).astype(jnp.bfloat16).astype(jnp.float32)
    query_grad = jnp.einsum('nhqk,nkhc->nqhc', score_grad, keys_in)
    key_grad = jnp.einsum('nhqk,nqhc->nkhc', score_grad, queries)
    joint_grad = jnp.concatenate([query_grad.reshape(row_count, D), key_grad.reshape(row_count, D), value_grad.reshape(row_count, D)], axis=1).astype(jnp.bfloat16)
    attend_g = jnp.dot(stored['normed_one'].T, joint_grad, preferred_element_type=jnp.float32)
    normed_one_grad = jnp.dot(joint_grad, attend_w.T, preferred_element_type=jnp.float32)
    pull_one = jax.vjp(norm_apply, stored['inputs'], gain_rows[0].astype(jnp.float32), bias_rows[0].astype(jnp.float32))[1]
    input_part, gain_one, bias_one = pull_one(normed_one_grad)
    input_grad = hidden_grad + input_part
    grad_set = (jnp.stack([gain_one, gain_two]), jnp.stack([bias_one, bias_two]), attend_g, output_g, router_g, first_all, second_all)
    return (input_grad, grad_set)

def reference(boundary, routes, norm_gains, norm_biases, attend_weight, output_weight, router_weight, expert_in, expert_out):
    layer_params = []
    for section_no in range(2):
        layer_params.append((norm_gains[section_no], norm_biases[section_no], attend_weight[section_no], output_weight[section_no], router_weight[section_no], expert_in[section_no], expert_out[section_no]))
    totals = [None, None]
    input_grads = []
    outputs = []
    for micro_no in range(M):
        first_out, first_kept = layer_forward(layer_params[0], boundary[0, micro_no], routes[0, micro_no])
        passed = first_out.astype(jnp.bfloat16).reshape(IMAGES_MB, S, D)
        second_out, second_kept = layer_forward(layer_params[1], passed, routes[1, micro_no])
        outputs.append(second_out.astype(jnp.bfloat16).reshape(IMAGES_MB, S, D))
        cotangent = boundary[1, micro_no].reshape(-1, D).astype(jnp.float32)
        second_in, second_grads = layer_backward(layer_params[1], second_kept, cotangent)
        sent_back = lax.optimization_barrier(second_in.astype(jnp.bfloat16)).astype(jnp.float32)
        first_in, first_grads = layer_backward(layer_params[0], first_kept, sent_back)
        input_grads.append(first_in.astype(jnp.bfloat16).reshape(IMAGES_MB, S, D))
        for section_no, grad_set in ((0, first_grads), (1, second_grads)):
            if totals[section_no] is None:
                totals[section_no] = grad_set
            else:
                totals[section_no] = tuple((summand + extra for summand, extra in zip(totals[section_no], grad_set)))
    results = jnp.stack([jnp.stack(input_grads), jnp.stack(outputs)])
    stacked = [jnp.stack([totals[0][index_no], totals[1][index_no]]) for index_no in range(7)]
    return (results, stacked[0], stacked[1], stacked[2], stacked[3], stacked[4], stacked[5], stacked[6])
```

```python
import functools
import math

import jax
import jax.numpy as jnp
from jax import lax
from jax.experimental import pallas as pl
from jax.experimental.pallas import tpu as pltpu
from jax.sharding import PartitionSpec as P

D = 768
HEADS = 12
HEAD_DIM = 64
S = 50
EPSILON = 1e-06
PACKED = 3200
BF = jnp.bfloat16
F32 = jnp.float32


def mm(left, right):
    return jnp.dot(left, right, preferred_element_type=F32)


def ein(spec, *args):
    return jnp.einsum(spec, *args, preferred_element_type=F32)


def norm_apply(inputs, gain_vec, bias_vec):
    centre = jnp.mean(inputs, axis=-1, keepdims=True)
    spread = jnp.mean(jnp.square(inputs - centre), axis=-1, keepdims=True)
    return (inputs - centre) * lax.rsqrt(spread + EPSILON) * gain_vec + bias_vec


def gelu_tanh(pre_act):
    return jax.nn.gelu(pre_act, approximate=True)


def handed(value, by):
    length = lax.axis_size("section")
    pairs = [(i, i + by) for i in range(length) if 0 <= i + by < length]
    return lax.ppermute(value, "section", pairs)


def route_tables(routes, experts, groups, capacity, block):
    micro, rows, _ = routes.shape
    local = experts // groups
    share = block // local + 2
    flat = routes.reshape(micro, rows * 2)
    onehot = (flat[:, :, None] == jnp.arange(experts, dtype=jnp.int32)).astype(BF)
    order = jnp.arange(rows * 2, dtype=jnp.int32)
    earlier = (order[None, :] < order[:, None]).astype(BF)
    before = ein("ab,mbe->mae", earlier, onehot)
    slot = jnp.sum(before * onehot.astype(F32), axis=-1).astype(jnp.int32)
    micro_at = jnp.arange(micro, dtype=jnp.int32)[:, None]
    target = (flat // local) * block + (flat % local) * share + micro_at * capacity + slot
    target = target.reshape(micro * rows, 2)
    places = jnp.arange(groups * block, dtype=jnp.int32)[:, None]
    pick_first = (target[None, :, 0] == places).astype(BF)
    pick_second = (target[None, :, 1] == places).astype(BF)
    onehot = onehot.reshape(micro * rows, 2, experts).astype(F32)
    return onehot[:, 0], onehot[:, 1], pick_first, pick_second


MESH = pl.DeviceIdType.MESH
RING = 4


def peer_at(me, step):
    row, column = me // RING, me % RING
    return (row + step // RING) % RING * RING + (column + step % RING) % RING


def origin_at(me, step):
    row, column = me // RING, me % RING
    return (row + RING - step // RING) % RING * RING + (column + RING - step % RING) % RING


def greet(me, partner, across, groups):
    barrier = pltpu.get_barrier_semaphore()

    def one(step, carry):
        pl.semaphore_signal(barrier, inc=1, device_id={"expert": peer_at(me, step)}, device_id_type=MESH)
        return carry

    lax.fori_loop(1, groups, one, 0)
    pl.semaphore_signal(barrier, inc=1, device_id={"replica": partner}, device_id_type=MESH)
    pl.semaphore_signal(barrier, inc=1, device_id={"replica": across}, device_id_type=MESH)
    pl.semaphore_wait(barrier, groups + 1)


def remote(source, target, sems, step, device):
    return pltpu.make_async_remote_copy(
        src_ref=source, dst_ref=target, send_sem=sems[0].at[step], recv_sem=sems[1].at[step],
        device_id=device, device_id_type=MESH,
    )


def spread_kernel(groups, send, out, swap_s, swap_r, near_s, near_r, far_s, far_r, last_s, last_r, own_sem):
    me, rep = lax.axis_index("expert"), lax.axis_index("replica")
    partner = rep + 1 - 2 * (rep % 2)
    across = (rep + 2) % 4
    greet(me, partner, across, groups)

    def swap(step):
        there = peer_at(me, step)
        return remote(send.at[there], out.at[rep, me], (swap_s, swap_r), step, {"expert": there})

    def near(step, block):
        from_at = origin_at(me, step)
        return remote(block, out.at[rep, from_at], (near_s, near_r), step, {"replica": partner})

    def far(step, block):
        from_at = origin_at(me, step)
        return remote(block, out.at[rep, from_at], (far_s, far_r), step, {"replica": across})

    def last(step):
        from_at = origin_at(me, step)
        return remote(out.at[across, from_at], out.at[across, from_at], (last_s, last_r), step, {"replica": partner})

    far(0, send.at[me]).start()
    near(0, send.at[me]).start()
    keep = pltpu.make_async_copy(send.at[me], out.at[rep, me], own_sem)
    keep.start()

    def first(step, carry):
        swap(step).start()
        return carry

    lax.fori_loop(1, groups, first, 0)

    def pass_on(step, carry):
        swap(step).wait_recv()
        block = out.at[rep, origin_at(me, step)]
        far(step, block).start()
        near(step, block).start()
        return carry

    lax.fori_loop(1, groups, pass_on, 0)

    def pass_last(step, carry):
        far(step, send.at[me]).wait_recv()
        last(step).start()
        return carry

    lax.fori_loop(0, groups, pass_last, 0)

    def finish(step, carry):
        near(step, send.at[me]).wait()
        far(step, send.at[me]).wait_send()
        last(step).wait()
        return carry

    lax.fori_loop(0, groups, finish, 0)

    def sent(step, carry):
        swap(step).wait_send()
        return carry

    lax.fori_loop(1, groups, sent, 0)
    keep.wait()


def spread_rows(sending):
    groups, block, _ = sending.shape
    out = pl.pallas_call(
        functools.partial(spread_kernel, groups),
        out_shape=jax.ShapeDtypeStruct((4,) + sending.shape, sending.dtype),
        in_specs=[pl.BlockSpec(memory_space=pltpu.VMEM)],
        out_specs=pl.BlockSpec(memory_space=pl.ANY),
        scratch_shapes=[pltpu.SemaphoreType.DMA((groups,))] * 8 + [pltpu.SemaphoreType.DMA],
        compiler_params=pltpu.CompilerParams(collective_id=0, has_side_effects=True),
        name="spread_rows",
    )(sending)
    return out.reshape(4 * groups, block, D)


def return_kernel(groups, part, out, near_in, far_in, pair, total, near_s, near_r, far_s, far_r, home_s, home_r, own_sem):
    me, rep = lax.axis_index("expert"), lax.axis_index("replica")
    partner = rep + 1 - 2 * (rep % 2)
    across = (rep + 2) % 4
    partner_across = (partner + 2) % 4
    greet(me, partner, across, groups)

    def near(side, step):
        whose = partner_across if side == 0 else partner
        return remote(
            part.at[whose, peer_at(me, step)], near_in.at[side, step],
            (near_s.at[side], near_r.at[side]), step, {"replica": partner},
        )

    def far(step):
        return remote(pair.at[step], far_in.at[step], (far_s, far_r), step, {"replica": across})

    def home(step):
        return remote(total.at[step], out.at[me], (home_s, home_r), step, {"expert": peer_at(me, step)})

    for side in range(2):

        def send_near(step, carry, side=side):
            near(side, step).start()
            return carry

        lax.fori_loop(0, groups, send_near, 0)

    def send_far(step, carry):
        near(0, step).wait_recv()
        both = part[across, peer_at(me, step)].astype(F32) + near_in[0, step].astype(F32)
        pair[step] = both.astype(BF)
        far(step).start()
        return carry

    lax.fori_loop(0, groups, send_far, 0)

    def close(step):
        near(1, step).wait_recv()
        far(step).wait_recv()
        whole = part[rep, peer_at(me, step)].astype(F32) + near_in[1, step].astype(F32) + far_in[step].astype(F32)
        total[step] = whole.astype(BF)

    close(0)
    keep = pltpu.make_async_copy(total.at[0], out.at[me], own_sem)
    keep.start()

    def send_home(step, carry):
        close(step)
        home(step).start()
        return carry

    lax.fori_loop(1, groups, send_home, 0)

    def finish(step, carry):
        home(step).wait()
        return carry

    lax.fori_loop(1, groups, finish, 0)

    def sent(step, carry):
        near(0, step).wait_send()
        near(1, step).wait_send()
        far(step).wait_send()
        return carry

    lax.fori_loop(0, groups, sent, 0)
    keep.wait()


def return_rows(partial_rows):
    sources, block, _ = partial_rows.shape
    groups = sources // 4
    shape = (groups, block, D)
    out = pl.pallas_call(
        functools.partial(return_kernel, groups),
        out_shape=jax.ShapeDtypeStruct(shape, BF),
        in_specs=[pl.BlockSpec(memory_space=pltpu.VMEM)],
        out_specs=pl.BlockSpec(memory_space=pltpu.VMEM),
        scratch_shapes=[
            pltpu.VMEM((2,) + shape, BF), pltpu.VMEM(shape, BF), pltpu.VMEM(shape, BF), pltpu.VMEM(shape, BF),
            pltpu.SemaphoreType.DMA((2, groups)), pltpu.SemaphoreType.DMA((2, groups)),
        ] + [pltpu.SemaphoreType.DMA((groups,))] * 4 + [pltpu.SemaphoreType.DMA],
        compiler_params=pltpu.CompilerParams(collective_id=1, has_side_effects=True),
        name="return_rows",
    )(partial_rows.reshape(4, groups, block, D))
    return out.reshape(groups * block, D)


def by_expert(rows):
    sources, block, _ = rows.shape
    window = 24
    at = jnp.arange(window, dtype=jnp.int32)[None, :, None]
    low = jnp.where(at < block // 2, rows[:, :window], 0)
    high = jnp.where(at >= window - block // 2, rows[:, block - window :], 0)
    return jnp.stack([low, high]).reshape(2, sources * window, D)


def from_expert(windows, block):
    window = 24
    shaped = windows.reshape(2, -1, window, D)
    edge = block - window
    return jnp.concatenate(
        [shaped[0, :, :edge], shaped[0, :, edge:] + shaped[1, :, : window - edge], shaped[1, :, window - edge :]], axis=1
    ).astype(BF)


def attention_inputs(joint, images):
    shaped = joint.reshape(images, S, 3, HEADS, HEAD_DIM)
    return shaped[:, :, 0], shaped[:, :, 1], shaped[:, :, 2]


def layer_forward(dense, experts, tables, tokens):
    gain, bias, attend_w, output_w, router_w = dense
    weight_in, weight_out = experts
    hot_first, hot_second, pick_first, pick_second = tables
    rows = tokens.shape[0]
    images = rows // S
    scaling = 1.0 / math.sqrt(HEAD_DIM)
    groups = lax.axis_size("expert")
    inputs = tokens.astype(F32)
    normed_one = norm_apply(inputs, gain[0], bias[0]).astype(BF)
    joint = mm(normed_one, attend_w).astype(BF)
    queries, keys, values = attention_inputs(joint, images)
    scores = ein("nqhc,nkhc->nhqk", queries, keys) * scaling
    row_max = jnp.max(scores, axis=-1, keepdims=True)
    raised = jnp.exp(scores - row_max)
    row_total = jnp.sum(raised, axis=-1, keepdims=True)
    log_total = row_max + jnp.log(row_total)
    prob = (raised / row_total).astype(BF)
    mixed = ein("nhqk,nkhc->nqhc", prob, values).reshape(rows, D).astype(BF)
    hidden = inputs + mm(mixed, output_w)
    normed_two = norm_apply(hidden, gain[1], bias[1]).astype(BF)
    logits = mm(normed_two, router_w)
    chosen = jnp.stack([jnp.sum(logits * hot_first, -1), jnp.sum(logits * hot_second, -1)], axis=1)
    gates = jax.nn.softmax(chosen, axis=-1)
    sending = mm(pick_first + pick_second, normed_two).astype(BF).reshape(groups, -1, D)
    received = spread_rows(sending)
    shaped = by_expert(received)
    pre_act = ein("esd,edh->esh", shaped, weight_in)
    active = gelu_tanh(pre_act).astype(BF)
    partial = ein("esh,ehd->esd", active, weight_out)
    returned = return_rows(from_expert(partial, received.shape[1]))
    first_rows = ein("pr,pd->rd", pick_first, returned)
    second_rows = ein("pr,pd->rd", pick_second, returned)
    output = hidden + (gates[:, 0:1] * first_rows + gates[:, 1:2] * second_rows)
    stored = dict(
        inputs=inputs, normed_one=normed_one, joint=joint, log_total=log_total, mixed=mixed,
        hidden=hidden, normed_two=normed_two, gates=gates, first_rows=first_rows.astype(BF),
        second_rows=second_rows.astype(BF), received=shaped, pre_act=pre_act, active=active,
    )
    return output, stored


def layer_backward(dense, experts, tables, stored, cotangent):
    gain, bias, attend_w, output_w, router_w = dense
    weight_in, weight_out = experts
    hot_first, hot_second, pick_first, pick_second = tables
    rows = cotangent.shape[0]
    images = rows // S
    scaling = 1.0 / math.sqrt(HEAD_DIM)
    groups = lax.axis_size("expert")
    gates = stored["gates"]
    first_send = (gates[:, 0:1] * cotangent).astype(BF)
    second_send = (gates[:, 1:2] * cotangent).astype(BF)
    grad_send = mm(pick_first, first_send) + mm(pick_second, second_send)
    grad_all = spread_rows(grad_send.astype(BF).reshape(groups, -1, D))
    gate_grad = jnp.stack(
        [
            jnp.sum(cotangent * stored["first_rows"].astype(F32), axis=-1),
            jnp.sum(cotangent * stored["second_rows"].astype(F32), axis=-1),
        ],
        axis=1,
    )
    chosen_grad = gates * (gate_grad - jnp.sum(gates * gate_grad, axis=-1, keepdims=True))
    logit_grad = (chosen_grad[:, 0:1] * hot_first + chosen_grad[:, 1:2] * hot_second).astype(BF)
    router_g = mm(stored["normed_two"].T, logit_grad)
    router_part = mm(logit_grad, router_w.T)
    grad_shaped = by_expert(grad_all)
    act_grad = ein("esd,ehd->esh", grad_shaped, weight_out)
    pre_grad = jax.vjp(gelu_tanh, stored["pre_act"])[1](act_grad)[0].astype(BF)
    back_part = ein("esh,edh->esd", pre_grad, weight_in)
    back_home = return_rows(from_expert(back_part, grad_all.shape[1]))
    both_back = mm((pick_first + pick_second).T, back_home)
    normed_grad = router_part + both_back
    pull_two = jax.vjp(norm_apply, stored["hidden"], gain[1], bias[1])[1]
    hidden_part, gain_two, bias_two = pull_two(normed_grad)
    hidden_grad = cotangent + hidden_part
    hidden_b = hidden_grad.astype(BF)
    output_g = mm(stored["mixed"].T, hidden_b)
    mixed_grad = mm(hidden_b, output_w.T).astype(BF).reshape(images, S, HEADS, HEAD_DIM)
    queries, keys, values = attention_inputs(stored["joint"], images)
    scores = ein("nqhc,nkhc->nhqk", queries, keys) * scaling
    prob = jnp.exp(scores - stored["log_total"])
    value_grad = ein("nhqk,nqhc->nkhc", prob.astype(BF), mixed_grad)
    prob_grad = ein("nqhc,nkhc->nhqk", mixed_grad, values)
    row_delta = jnp.sum(prob * prob_grad, axis=-1, keepdims=True)
    score_grad = (prob * (prob_grad - row_delta) * scaling).astype(BF)
    query_grad = ein("nhqk,nkhc->nqhc", score_grad, keys)
    key_grad = ein("nhqk,nqhc->nkhc", score_grad, queries)
    joint_grad = jnp.concatenate(
        [query_grad.reshape(rows, D), key_grad.reshape(rows, D), value_grad.reshape(rows, D)], axis=1
    ).astype(BF)
    attend_g = mm(stored["normed_one"].T, joint_grad)
    normed_one_grad = mm(joint_grad, attend_w.T)
    pull_one = jax.vjp(norm_apply, stored["inputs"], gain[0], bias[0])[1]
    input_part, gain_one, bias_one = pull_one(normed_one_grad)
    input_grad = hidden_grad + input_part
    dense_grads = (jnp.stack([gain_one, gain_two]), jnp.stack([bias_one, bias_two]), attend_g, output_g, router_g)
    expert_grads = (
        ein("esd,esh->edh", stored["received"], pre_grad),
        ein("esh,esd->ehd", stored["active"], grad_shaped),
    )
    return input_grad, dense_grads, expert_grads


def packed(gain, bias, attend, output, router):
    joined = jnp.concatenate([attend, output, router, gain.T, bias.T], axis=1)
    return jnp.pad(joined, ((0, 0), (0, PACKED - joined.shape[1])))


def unpacked(joined, experts):
    at = [3 * D, 4 * D, 4 * D + experts, 4 * D + experts + 2, 4 * D + experts + 4]
    return (
        joined[:, at[2] : at[3]].T,
        joined[:, at[3] : at[4]].T,
        joined[:, : at[0]],
        joined[:, at[0] : at[1]],
        joined[:, at[1] : at[2]],
    )


def shards(
    boundary, routes, norm_gains, norm_biases, attend_weight, output_weight, router_weight, expert_in, expert_out
):
    section_at = lax.axis_index("section")
    micro = boundary.shape[1]
    rows = boundary.shape[2] * boundary.shape[3]
    own = boundary[0].reshape(micro * rows, D)
    total_experts = router_weight.shape[2]
    groups = lax.axis_size("expert")
    capacity = 9
    block = 40
    tables = route_tables(routes[0].reshape(micro, rows, 2), total_experts, groups, capacity, block)
    experts = (expert_in[0], expert_out[0])
    gathered = lax.all_gather(
        packed(norm_gains[0], norm_biases[0], attend_weight[0], output_weight[0], router_weight[0]),
        "expert", axis=0, tiled=True,
    )
    gain, bias, attend_w, output_w, router_w = unpacked(gathered, total_experts)
    dense = (gain.astype(F32), bias.astype(F32), attend_w, output_w, router_w)

    first_out, _ = layer_forward(dense, experts, tables, own)
    incoming = handed(first_out.astype(BF), 1)
    tokens = jnp.where(section_at == 0, own, incoming)
    final_out, stored = layer_forward(dense, experts, tables, tokens)
    first_back, _, _ = layer_backward(dense, experts, tables, stored, own.astype(F32))
    incoming_back = handed(first_back.astype(BF), -1)
    cotangent = jnp.where(section_at == 1, own, incoming_back).astype(F32)
    input_grad, dense_grads, expert_grads = layer_backward(dense, experts, tables, stored, cotangent)

    mine = packed(*dense_grads).astype(BF)
    owned = lax.psum_scatter(mine, "expert", scatter_dimension=0, tiled=True)
    owned = lax.psum(owned, "replica").astype(F32)
    gain_g, bias_g, attend_g, output_g, router_g = unpacked(owned, total_experts)
    merged = jnp.where(section_at == 0, input_grad.astype(BF), final_out.astype(BF)).reshape(boundary.shape)
    return (
        merged, gain_g[None], bias_g[None], attend_g[None], output_g[None], router_g[None],
        expert_grads[0][None], expert_grads[1][None],
    )


def solution(mesh):
    in_specs = (
        P("section", None, ("expert", "replica"), None, None),
        P("section", None, ("expert", "replica"), None, None),
        P("section", None, "expert"),
        P("section", None, "expert"),
        P("section", "expert", None),
        P("section", "expert", None),
        P("section", "expert", None),
        P("section", "expert", None, "replica"),
        P("section", "expert", "replica", None),
    )
    out_specs = in_specs[:1] + in_specs[2:]
    return jax.shard_map(shards, mesh=mesh, in_specs=in_specs, out_specs=out_specs, check_vma=False)
```

```python
import functools
import math

import jax
import jax.numpy as jnp
from jax import lax
from jax.experimental import pallas as pl
from jax.experimental.pallas import tpu as pltpu
from jax.sharding import PartitionSpec as P

D = 768
HEADS = 12
HEAD_DIM = 64
S = 50
EPSILON = 1e-06
BF = jnp.bfloat16
F32 = jnp.float32


def mm(left, right):
    return jnp.dot(left, right, preferred_element_type=F32)


def ein(spec, *args):
    return jnp.einsum(spec, *args, preferred_element_type=F32)


def norm_apply(inputs, gain_vec, bias_vec):
    centre = jnp.mean(inputs, axis=-1, keepdims=True)
    spread = jnp.mean(jnp.square(inputs - centre), axis=-1, keepdims=True)
    return (inputs - centre) * lax.rsqrt(spread + EPSILON) * gain_vec + bias_vec


def gelu_tanh(pre_act):
    return jax.nn.gelu(pre_act, approximate=True)


def handed(value, by):
    length = lax.axis_size("section")
    pairs = [(i, i + by) for i in range(length) if 0 <= i + by < length]
    return lax.ppermute(value, "section", pairs)


def route_tables(routes, experts, groups, capacity, block):
    micro, rows, _ = routes.shape
    local = experts // groups
    share = block // local + 2
    flat = routes.reshape(micro, rows * 2)
    onehot = (flat[:, :, None] == jnp.arange(experts, dtype=jnp.int32)).astype(BF)
    order = jnp.arange(rows * 2, dtype=jnp.int32)
    earlier = (order[None, :] < order[:, None]).astype(BF)
    before = ein("ab,mbe->mae", earlier, onehot)
    slot = jnp.sum(before * onehot.astype(F32), axis=-1).astype(jnp.int32)
    micro_at = jnp.arange(micro, dtype=jnp.int32)[:, None]
    target = (flat // local) * block + (flat % local) * share + micro_at * capacity + slot
    target = target.reshape(micro * rows, 2)
    places = jnp.arange(groups * block, dtype=jnp.int32)[:, None]
    pick_first = (target[None, :, 0] == places).astype(BF)
    pick_second = (target[None, :, 1] == places).astype(BF)
    onehot = onehot.reshape(micro * rows, 2, experts).astype(F32)
    return onehot[:, 0], onehot[:, 1], pick_first, pick_second


MESH = pl.DeviceIdType.MESH
RING = 4


def peer_at(me, step):
    row, column = me // RING, me % RING
    return (row + step // RING) % RING * RING + (column + step % RING) % RING


def origin_at(me, step):
    row, column = me // RING, me % RING
    return (row + RING - step // RING) % RING * RING + (column + RING - step % RING) % RING


def greet(me, partner, across, groups):
    barrier = pltpu.get_barrier_semaphore()

    def one(step, carry):
        pl.semaphore_signal(barrier, inc=1, device_id={"expert": peer_at(me, step)}, device_id_type=MESH)
        return carry

    lax.fori_loop(1, groups, one, 0)
    pl.semaphore_signal(barrier, inc=1, device_id={"replica": partner}, device_id_type=MESH)
    pl.semaphore_signal(barrier, inc=1, device_id={"replica": across}, device_id_type=MESH)
    pl.semaphore_wait(barrier, groups + 1)


def remote(source, target, sems, step, device):
    return pltpu.make_async_remote_copy(
        src_ref=source, dst_ref=target, send_sem=sems[0].at[step], recv_sem=sems[1].at[step],
        device_id=device, device_id_type=MESH,
    )


def spread_kernel(groups, send, out, swap_s, swap_r, near_s, near_r, far_s, far_r, last_s, last_r, own_sem):
    me, rep = lax.axis_index("expert"), lax.axis_index("replica")
    partner = rep + 1 - 2 * (rep % 2)
    across = (rep + 2) % 4
    greet(me, partner, across, groups)

    def swap(step):
        there = peer_at(me, step)
        return remote(send.at[there], out.at[rep, me], (swap_s, swap_r), step, {"expert": there})

    def near(step, block):
        from_at = origin_at(me, step)
        return remote(block, out.at[rep, from_at], (near_s, near_r), step, {"replica": partner})

    def far(step, block):
        from_at = origin_at(me, step)
        return remote(block, out.at[rep, from_at], (far_s, far_r), step, {"replica": across})

    def last(step):
        from_at = origin_at(me, step)
        return remote(out.at[across, from_at], out.at[across, from_at], (last_s, last_r), step, {"replica": partner})

    far(0, send.at[me]).start()
    near(0, send.at[me]).start()
    keep = pltpu.make_async_copy(send.at[me], out.at[rep, me], own_sem)
    keep.start()

    def first(step, carry):
        swap(step).start()
        return carry

    lax.fori_loop(1, groups, first, 0)

    def pass_on(step, carry):
        swap(step).wait_recv()
        block = out.at[rep, origin_at(me, step)]
        far(step, block).start()
        near(step, block).start()
        return carry

    lax.fori_loop(1, groups, pass_on, 0)

    def pass_last(step, carry):
        far(step, send.at[me]).wait_recv()
        last(step).start()
        return carry

    lax.fori_loop(0, groups, pass_last, 0)

    def finish(step, carry):
        near(step, send.at[me]).wait()
        far(step, send.at[me]).wait_send()
        last(step).wait()
        return carry

    lax.fori_loop(0, groups, finish, 0)

    def sent(step, carry):
        swap(step).wait_send()
        return carry

    lax.fori_loop(1, groups, sent, 0)
    keep.wait()


def spread_rows(sending):
    groups, block, _ = sending.shape
    out = pl.pallas_call(
        functools.partial(spread_kernel, groups),
        out_shape=jax.ShapeDtypeStruct((4,) + sending.shape, sending.dtype),
        in_specs=[pl.BlockSpec(memory_space=pltpu.VMEM)],
        out_specs=pl.BlockSpec(memory_space=pl.ANY),
        scratch_shapes=[pltpu.SemaphoreType.DMA((groups,))] * 8 + [pltpu.SemaphoreType.DMA],
        compiler_params=pltpu.CompilerParams(collective_id=0, has_side_effects=True),
        name="spread_rows",
    )(sending)
    return out.reshape(4 * groups, block, D)


def return_kernel(groups, part, out, near_in, far_in, pair, total, near_s, near_r, far_s, far_r, home_s, home_r, own_sem):
    me, rep = lax.axis_index("expert"), lax.axis_index("replica")
    partner = rep + 1 - 2 * (rep % 2)
    across = (rep + 2) % 4
    partner_across = (partner + 2) % 4
    greet(me, partner, across, groups)

    def near(side, step):
        whose = partner_across if side == 0 else partner
        return remote(
            part.at[whose, peer_at(me, step)], near_in.at[side, step],
            (near_s.at[side], near_r.at[side]), step, {"replica": partner},
        )

    def far(step):
        return remote(pair.at[step], far_in.at[step], (far_s, far_r), step, {"replica": across})

    def home(step):
        return remote(total.at[step], out.at[me], (home_s, home_r), step, {"expert": peer_at(me, step)})

    for side in range(2):

        def send_near(step, carry, side=side):
            near(side, step).start()
            return carry

        lax.fori_loop(0, groups, send_near, 0)

    def send_far(step, carry):
        near(0, step).wait_recv()
        both = part[across, peer_at(me, step)].astype(F32) + near_in[0, step].astype(F32)
        pair[step] = both.astype(BF)
        far(step).start()
        return carry

    lax.fori_loop(0, groups, send_far, 0)

    def close(step):
        near(1, step).wait_recv()
        far(step).wait_recv()
        whole = part[rep, peer_at(me, step)].astype(F32) + near_in[1, step].astype(F32) + far_in[step].astype(F32)
        total[step] = whole.astype(BF)

    close(0)
    keep = pltpu.make_async_copy(total.at[0], out.at[me], own_sem)
    keep.start()

    def send_home(step, carry):
        close(step)
        home(step).start()
        return carry

    lax.fori_loop(1, groups, send_home, 0)

    def finish(step, carry):
        home(step).wait()
        return carry

    lax.fori_loop(1, groups, finish, 0)

    def sent(step, carry):
        near(0, step).wait_send()
        near(1, step).wait_send()
        far(step).wait_send()
        return carry

    lax.fori_loop(0, groups, sent, 0)
    keep.wait()


def return_rows(partial_rows):
    sources, block, _ = partial_rows.shape
    groups = sources // 4
    shape = (groups, block, D)
    out = pl.pallas_call(
        functools.partial(return_kernel, groups),
        out_shape=jax.ShapeDtypeStruct(shape, BF),
        in_specs=[pl.BlockSpec(memory_space=pltpu.VMEM)],
        out_specs=pl.BlockSpec(memory_space=pltpu.VMEM),
        scratch_shapes=[
            pltpu.VMEM((2,) + shape, BF), pltpu.VMEM(shape, BF), pltpu.VMEM(shape, BF), pltpu.VMEM(shape, BF),
            pltpu.SemaphoreType.DMA((2, groups)), pltpu.SemaphoreType.DMA((2, groups)),
        ] + [pltpu.SemaphoreType.DMA((groups,))] * 4 + [pltpu.SemaphoreType.DMA],
        compiler_params=pltpu.CompilerParams(collective_id=1, has_side_effects=True),
        name="return_rows",
    )(partial_rows.reshape(4, groups, block, D))
    return out.reshape(groups * block, D)


def by_expert(rows):
    sources, block, _ = rows.shape
    window = 24
    at = jnp.arange(window, dtype=jnp.int32)[None, :, None]
    low = jnp.where(at < block // 2, rows[:, :window], 0)
    high = jnp.where(at >= window - block // 2, rows[:, block - window :], 0)
    return jnp.stack([low, high]).reshape(2, sources * window, D)


def from_expert(windows, block):
    window = 24
    shaped = windows.reshape(2, -1, window, D)
    edge = block - window
    return jnp.concatenate(
        [shaped[0, :, :edge], shaped[0, :, edge:] + shaped[1, :, : window - edge], shaped[1, :, window - edge :]], axis=1
    ).astype(BF)


def attention_inputs(joint, images):
    shaped = joint.reshape(images, S, 3, HEADS, HEAD_DIM)
    return shaped[:, :, 0], shaped[:, :, 1], shaped[:, :, 2]


def layer_forward(dense, experts, tables, tokens):
    gain, bias, attend_w, output_w, router_w = dense
    weight_in, weight_out = experts
    hot_first, hot_second, pick_first, pick_second = tables
    rows = tokens.shape[0]
    images = rows // S
    scaling = 1.0 / math.sqrt(HEAD_DIM)
    groups = lax.axis_size("expert")
    inputs = tokens.astype(F32)
    normed_one = norm_apply(inputs, gain[0], bias[0]).astype(BF)
    joint = mm(normed_one, attend_w).astype(BF)
    queries, keys, values = attention_inputs(joint, images)
    scores = ein("nqhc,nkhc->nhqk", queries, keys) * scaling
    row_max = jnp.max(scores, axis=-1, keepdims=True)
    raised = jnp.exp(scores - row_max)
    row_total = jnp.sum(raised, axis=-1, keepdims=True)
    log_total = row_max + jnp.log(row_total)
    prob = (raised / row_total).astype(BF)
    mixed = ein("nhqk,nkhc->nqhc", prob, values).reshape(rows, D).astype(BF)
    hidden = inputs + mm(mixed, output_w)
    normed_two = norm_apply(hidden, gain[1], bias[1]).astype(BF)
    logits = mm(normed_two, router_w)
    chosen = jnp.stack([jnp.sum(logits * hot_first, -1), jnp.sum(logits * hot_second, -1)], axis=1)
    gates = jax.nn.softmax(chosen, axis=-1)
    sending = mm(pick_first + pick_second, normed_two).astype(BF).reshape(groups, -1, D)
    received = spread_rows(sending)
    shaped = by_expert(received)
    pre_act = ein("esd,edh->esh", shaped, weight_in)
    active = gelu_tanh(pre_act).astype(BF)
    partial = ein("esh,ehd->esd", active, weight_out)
    returned = return_rows(from_expert(partial, received.shape[1]))
    first_rows = ein("pr,pd->rd", pick_first, returned)
    second_rows = ein("pr,pd->rd", pick_second, returned)
    output = hidden + (gates[:, 0:1] * first_rows + gates[:, 1:2] * second_rows)
    stored = dict(
        inputs=inputs, normed_one=normed_one, joint=joint, log_total=log_total, mixed=mixed,
        hidden=hidden, normed_two=normed_two, gates=gates, first_rows=first_rows.astype(BF),
        second_rows=second_rows.astype(BF), received=shaped, pre_act=pre_act, active=active,
    )
    return output, stored


def layer_backward(dense, experts, tables, stored, cotangent):
    gain, bias, attend_w, output_w, router_w = dense
    weight_in, weight_out = experts
    hot_first, hot_second, pick_first, pick_second = tables
    rows = cotangent.shape[0]
    images = rows // S
    scaling = 1.0 / math.sqrt(HEAD_DIM)
    groups = lax.axis_size("expert")
    gates = stored["gates"]
    first_send = (gates[:, 0:1] * cotangent).astype(BF)
    second_send = (gates[:, 1:2] * cotangent).astype(BF)
    grad_send = mm(pick_first, first_send) + mm(pick_second, second_send)
    grad_all = spread_rows(grad_send.astype(BF).reshape(groups, -1, D))
    gate_grad = jnp.stack(
        [
            jnp.sum(cotangent * stored["first_rows"].astype(F32), axis=-1),
            jnp.sum(cotangent * stored["second_rows"].astype(F32), axis=-1),
        ],
        axis=1,
    )
    chosen_grad = gates * (gate_grad - jnp.sum(gates * gate_grad, axis=-1, keepdims=True))
    logit_grad = (chosen_grad[:, 0:1] * hot_first + chosen_grad[:, 1:2] * hot_second).astype(BF)
    router_g = mm(stored["normed_two"].T, logit_grad)
    router_part = mm(logit_grad, router_w.T)
    grad_shaped = by_expert(grad_all)
    act_grad = ein("esd,ehd->esh", grad_shaped, weight_out)
    pre_grad = jax.vjp(gelu_tanh, stored["pre_act"])[1](act_grad)[0].astype(BF)
    back_part = ein("esh,edh->esd", pre_grad, weight_in)
    back_home = return_rows(from_expert(back_part, grad_all.shape[1]))
    both_back = mm((pick_first + pick_second).T, back_home)
    normed_grad = router_part + both_back
    pull_two = jax.vjp(norm_apply, stored["hidden"], gain[1], bias[1])[1]
    hidden_part, gain_two, bias_two = pull_two(normed_grad)
    hidden_grad = cotangent + hidden_part
    hidden_b = hidden_grad.astype(BF)
    output_g = mm(stored["mixed"].T, hidden_b)
    mixed_grad = mm(hidden_b, output_w.T).astype(BF).reshape(images, S, HEADS, HEAD_DIM)
    queries, keys, values = attention_inputs(stored["joint"], images)
    scores = ein("nqhc,nkhc->nhqk", queries, keys) * scaling
    prob = jnp.exp(scores - stored["log_total"])
    value_grad = ein("nhqk,nqhc->nkhc", prob.astype(BF), mixed_grad)
    prob_grad = ein("nqhc,nkhc->nhqk", mixed_grad, values)
    row_delta = jnp.sum(prob * prob_grad, axis=-1, keepdims=True)
    score_grad = (prob * (prob_grad - row_delta) * scaling).astype(BF)
    query_grad = ein("nhqk,nkhc->nqhc", score_grad, keys)
    key_grad = ein("nhqk,nqhc->nkhc", score_grad, queries)
    joint_grad = jnp.concatenate(
        [query_grad.reshape(rows, D), key_grad.reshape(rows, D), value_grad.reshape(rows, D)], axis=1
    ).astype(BF)
    attend_g = mm(stored["normed_one"].T, joint_grad)
    normed_one_grad = mm(joint_grad, attend_w.T)
    pull_one = jax.vjp(norm_apply, stored["inputs"], gain[0], bias[0])[1]
    input_part, gain_one, bias_one = pull_one(normed_one_grad)
    input_grad = hidden_grad + input_part
    dense_grads = (jnp.stack([gain_one, gain_two]), jnp.stack([bias_one, bias_two]), attend_g, output_g, router_g)
    expert_grads = (
        ein("esd,esh->edh", stored["received"], pre_grad),
        ein("esh,esd->ehd", stored["active"], grad_shaped),
    )
    return input_grad, dense_grads, expert_grads


def along(half, me, first, second):
    row, column = me // RING, me % RING
    down, over = (first, second) if half == 0 else (second, first)
    return (row + down + RING) % RING * RING + (column + over + RING) % RING


def greet_lines(me, others):
    barrier = pltpu.get_barrier_semaphore()
    for step in range(1, RING):
        for half in range(2):
            pl.semaphore_signal(barrier, inc=1, device_id={"expert": along(half, me, step, 0)}, device_id_type=MESH)
    for other in others:
        pl.semaphore_signal(barrier, inc=1, device_id={"replica": other}, device_id_type=MESH)
    pl.semaphore_wait(barrier, 2 * (RING - 1) + len(others))


def gather_kernel(mine, out, hop_s, hop_r, near_s, near_r, own_sem):
    me, rep = lax.axis_index("expert"), lax.axis_index("replica")
    core = rep % 2
    partner = rep + 1 - 2 * core
    greet_lines(me, (partner,))

    def hop(half, first, second):
        index = first * RING + second
        from_at = along(half, me, 0, -second) if first else me
        source = mine.at[half, core] if from_at is me or second == 0 else out.at[half, from_at, core]
        there = along(half, me, first, 0) if first else along(half, me, 0, second)
        return remote(source, out.at[half, from_at, core], (hop_s.at[half], hop_r.at[half]), index, {"expert": there})

    def near(half, first, second):
        block = out.at[half, along(half, me, -first, -second), core]
        return remote(block, block, (near_s.at[half], near_r.at[half]), first * RING + second, {"replica": partner})

    keep = [pltpu.make_async_copy(mine.at[half], out.at[half, me], own_sem.at[half]) for half in range(2)]
    for half in range(2):
        for second in range(1, RING):
            hop(half, 0, second).start()
    for half in range(2):
        keep[half].start()
        for first in range(1, RING):
            hop(half, first, 0).start()
    for second in range(1, RING):
        for half in range(2):
            hop(half, 0, second).wait_recv()
            for first in range(1, RING):
                hop(half, first, second).start()
            near(half, 0, second).start()
    for second in range(RING):
        for first in range(1, RING):
            for half in range(2):
                hop(half, first, second).wait_recv()
                near(half, first, second).start()
    for half in range(2):
        keep[half].wait()
        for index in range(1, RING * RING):
            hop(half, index // RING, index % RING).wait_send()
            near(half, index // RING, index % RING).wait()


def gather_dense(mine):
    halves, rows, columns = mine.shape
    groups = RING * RING
    sems = [pltpu.SemaphoreType.DMA((halves, groups))] * 4 + [pltpu.SemaphoreType.DMA((halves,))]
    out = pl.pallas_call(
        gather_kernel,
        out_shape=jax.ShapeDtypeStruct((halves, groups, 2, rows // 2, columns), BF),
        in_specs=[pl.BlockSpec(memory_space=pltpu.VMEM)],
        out_specs=pl.BlockSpec(memory_space=pl.ANY),
        scratch_shapes=sems,
        compiler_params=pltpu.CompilerParams(collective_id=2, has_side_effects=True),
        name="gather_dense",
    )(mine.reshape(halves, 2, rows // 2, columns))
    return out.reshape(halves, groups * rows, columns)


def reduce_kernel(
    part, out, near_in, pair, one_in, one, two_in, mine, far_in, total, last_in,
    near_s, near_r, one_s, one_r, two_s, two_r, far_s, far_r, last_s, last_r,
):
    me, rep = lax.axis_index("expert"), lax.axis_index("replica")
    core = rep % 2
    partner = rep + 1 - 2 * core
    across = (rep + 2) % 4
    greet_lines(me, (partner, across))

    def near(half, index):
        there = along(half, me, index // RING, index % RING)
        return remote(
            part.at[half, there, 1 - core], near_in.at[half, index],
            (near_s.at[half], near_r.at[half]), index, {"replica": partner},
        )

    def stage_one(half, first):
        return remote(
            pair.at[half, pl.ds(first * RING, RING)], one_in.at[half, first - 1],
            (one_s.at[half], one_r.at[half]), first - 1, {"expert": along(half, me, first, 0)},
        )

    def stage_two(half, second):
        return remote(
            one.at[half, second], two_in.at[half, second - 1],
            (two_s.at[half], two_r.at[half]), second - 1, {"expert": along(half, me, 0, second)},
        )

    far = [remote(mine.at[half], far_in.at[half], (far_s, far_r), half, {"replica": across}) for half in range(2)]
    last = [remote(total.at[half], last_in.at[half], (last_s, last_r), half, {"replica": partner}) for half in range(2)]
    order = (1, 2, 3, 0)

    for first in order:
        for half in range(2):

            def send_near(second, carry, half=half, first=first):
                near(half, first * RING + second).start()
                return carry

            lax.fori_loop(0, RING, send_near, 0)
    for first in order:
        for half in range(2):

            def add_pair(second, carry, half=half, first=first):
                index = first * RING + second
                near(half, index).wait_recv()
                there = along(half, me, first, second)
                both = part[half, there, core].astype(F32) + near_in[half, index].astype(F32)
                pair[half, index] = both.astype(BF)
                return carry

            lax.fori_loop(0, RING, add_pair, 0)
            if first:
                stage_one(half, first).start()
    for half in range(2):
        for first in range(1, RING):
            stage_one(half, first).wait_recv()

        def add_one(second, carry, half=half):
            whole = pair[half, second].astype(F32)
            for first in range(1, RING):
                whole = whole + one_in[half, first - 1, second].astype(F32)
            one[half, second] = whole.astype(BF)
            return carry

        lax.fori_loop(0, RING, add_one, 0)
        for second in range(1, RING):
            stage_two(half, second).start()
    for half in range(2):
        whole = one[half, 0].astype(F32)
        for second in range(1, RING):
            stage_two(half, second).wait_recv()
            whole = whole + two_in[half, second - 1].astype(F32)
        mine[half] = whole.astype(BF)
        far[half].start()
    for half in range(2):
        far[half].wait_recv()
        total[half] = (mine[half].astype(F32) + far_in[half].astype(F32)).astype(BF)
        last[half].start()
        out[half, core] = total[half].astype(F32)
    for half in range(2):
        last[half].wait_recv()
        out[half, 1 - core] = last_in[half].astype(F32)
        last[half].wait_send()
        far[half].wait_send()
        for step in range(1, RING):
            stage_one(half, step).wait_send()
            stage_two(half, step).wait_send()

        def sent(index, carry, half=half):
            near(half, index).wait_send()
            return carry

        lax.fori_loop(0, RING * RING, sent, 0)


def reduce_dense(part):
    halves, depth, columns = part.shape
    groups = RING * RING
    rows = depth // groups // 2
    block = (rows, columns)
    out = pl.pallas_call(
        reduce_kernel,
        out_shape=jax.ShapeDtypeStruct((halves, 2) + block, F32),
        in_specs=[pl.BlockSpec(memory_space=pltpu.VMEM)],
        out_specs=pl.BlockSpec(memory_space=pltpu.VMEM),
        scratch_shapes=[
            pltpu.VMEM((halves, groups) + block, BF), pltpu.VMEM((halves, groups) + block, BF),
            pltpu.VMEM((halves, RING - 1, RING) + block, BF), pltpu.VMEM((halves, RING) + block, BF),
            pltpu.VMEM((halves, RING - 1) + block, BF), pltpu.VMEM((halves,) + block, BF),
            pltpu.VMEM((halves,) + block, BF), pltpu.VMEM((halves,) + block, BF), pltpu.VMEM((halves,) + block, BF),
        ] + [pltpu.SemaphoreType.DMA((halves, groups))] * 2 + [pltpu.SemaphoreType.DMA((halves, RING - 1))] * 4
        + [pltpu.SemaphoreType.DMA((halves,))] * 4,
        compiler_params=pltpu.CompilerParams(collective_id=3, has_side_effects=True),
        name="reduce_dense",
    )(part.reshape((halves, groups, 2) + block))
    return out.reshape(halves, 2 * rows, columns)


def packed(gain, bias, attend, output, router):
    edge = 2 * D
    low = jnp.concatenate([attend[:, :edge], router, gain.T, bias.T], axis=1)
    high = jnp.concatenate([attend[:, edge:], output], axis=1)
    return jnp.stack([jnp.pad(side, ((0, 0), (0, edge + 128 - side.shape[1]))) for side in (low, high)])


def unpacked(joined, experts):
    low, high = joined[0], joined[1]
    at = 2 * D + experts
    return (
        low[:, at : at + 2].T,
        low[:, at + 2 : at + 4].T,
        jnp.concatenate([low[:, : 2 * D], high[:, :D]], axis=1),
        high[:, D : 2 * D],
        low[:, 2 * D : at],
    )


def shards(
    boundary, routes, norm_gains, norm_biases, attend_weight, output_weight, router_weight, expert_in, expert_out
):
    section_at = lax.axis_index("section")
    micro = boundary.shape[1]
    rows = boundary.shape[2] * boundary.shape[3]
    own = boundary[0].reshape(micro * rows, D)
    total_experts = router_weight.shape[2]
    groups = lax.axis_size("expert")
    capacity = 9
    block = 40
    tables = route_tables(routes[0].reshape(micro, rows, 2), total_experts, groups, capacity, block)
    experts = (expert_in[0], expert_out[0])
    gathered = gather_dense(
        packed(norm_gains[0], norm_biases[0], attend_weight[0], output_weight[0], router_weight[0])
    )
    gain, bias, attend_w, output_w, router_w = unpacked(gathered, total_experts)
    dense = (gain.astype(F32), bias.astype(F32), attend_w, output_w, router_w)

    first_out, _ = layer_forward(dense, experts, tables, own)
    incoming = handed(first_out.astype(BF), 1)
    tokens = jnp.where(section_at == 0, own, incoming)
    final_out, stored = layer_forward(dense, experts, tables, tokens)
    first_back, _, _ = layer_backward(dense, experts, tables, stored, own.astype(F32))
    incoming_back = handed(first_back.astype(BF), -1)
    cotangent = jnp.where(section_at == 1, own, incoming_back).astype(F32)
    input_grad, dense_grads, expert_grads = layer_backward(dense, experts, tables, stored, cotangent)

    owned = reduce_dense(packed(*[grad.astype(BF) for grad in dense_grads]))
    gain_g, bias_g, attend_g, output_g, router_g = unpacked(owned, total_experts)
    merged = jnp.where(section_at == 0, input_grad.astype(BF), final_out.astype(BF)).reshape(boundary.shape)
    return (
        merged, gain_g[None], bias_g[None], attend_g[None], output_g[None], router_g[None],
        expert_grads[0][None], expert_grads[1][None],
    )


def solution(mesh):
    in_specs = (
        P("section", None, ("expert", "replica"), None, None),
        P("section", None, ("expert", "replica"), None, None),
        P("section", None, "expert"),
        P("section", None, "expert"),
        P("section", "expert", None),
        P("section", "expert", None),
        P("section", "expert", None),
        P("section", "expert", None, "replica"),
        P("section", "expert", "replica", None),
    )
    out_specs = in_specs[:1] + in_specs[2:]
    return jax.shard_map(shards, mesh=mesh, in_specs=in_specs, out_specs=out_specs, check_vma=False)
```
